32 devices in a mesh: dp: 8 (over z, y), ctx: 4 (over x, core).
Axes of the slice: x: 2, y: 2, z: 4, core: 2. Of those that a mesh axis runs over, the one named last changes fastest.
Arguments:
- queries: bfloat16 [8, 512, 4096], P('dp', 'ctx'), may hold values from -9 to 9
- keys: bfloat16 [8, 512, 512], P('dp', 'ctx'), may hold values from -7 to 7
- values: bfloat16 [8, 512, 512], P('dp', 'ctx'), may hold values from -6 to 6
- cotangent: bfloat16 [8, 512, 4096], P('dp', 'ctx'), may hold values from -6 to 6
- live: int32 [8, 512], P('dp', 'ctx'), may hold values from 0 to 1, as said below
- docs: int32 [8, 512], P('dp'), may hold values from 0 to 5, never falling along the last dimension, each value on 1 to 256 neighbouring positions
Outputs:
- attended: bfloat16 [8, 512, 4096], P('dp', 'ctx')
- grad_queries: bfloat16 [8, 512, 4096], P('dp', 'ctx')
- key_gradient: bfloat16 [8, 512, 512], P('dp', 'ctx')
- value_gradient: bfloat16 [8, 512, 512], P('dp', 'ctx')
The draws below stay inside these ranges and needn't reach their ends.
Inputs may be any that keep to these rules, and one draw needn't show every extreme that they name: `docs`: never falls along a sequence; each document spans 1 to 256 positions and one spans exactly 256. `live`: row 0 of every sequence is 1.
All inputs are finite; a program needn't handle non-finite values.
Results may differ from the reference program's by a relative error of at most 0.02.
Values may be sent and summed in bfloat16 or wider, within the bound.
A program may use at most 64 MiB of HBM per device.

```python
import math
import jax
import jax.numpy as jnp
import numpy as np
from jax import lax

QUERY_HEADS = 32
KEY_VALUE_HEADS = 4
HEAD_SIZE = 128
TOK_DEV = 128
DOCS = 6
SEQUENCE_TOKENS = 512
BATCH_SEQUENCES = 8
N_CTX = 4


def draw_queries(key, part):
    query_group_width = QUERY_HEADS // KEY_VALUE_HEADS
    array_shape = (BATCH_SEQUENCES, SEQUENCE_TOKENS, KEY_VALUE_HEADS, query_group_width, HEAD_SIZE)
    final_result = jnp.clip(jax.random.normal(jax.random.fold_in(key, 1), array_shape, jnp.float32), -6.0, 6.0)
    return final_result.reshape(BATCH_SEQUENCES, SEQUENCE_TOKENS, QUERY_HEADS * HEAD_SIZE).astype(jnp.bfloat16)


def draw_keys(key, part):
    array_shape = (BATCH_SEQUENCES, SEQUENCE_TOKENS, KEY_VALUE_HEADS, HEAD_SIZE)
    final_result = jnp.clip(jax.random.normal(jax.random.fold_in(key, 11), array_shape, jnp.float32), -6.0, 6.0)
    return final_result.reshape(BATCH_SEQUENCES, SEQUENCE_TOKENS, KEY_VALUE_HEADS * HEAD_SIZE).astype(jnp.bfloat16)


def draw_live(key, part):
    sequence_ids = jnp.arange(BATCH_SEQUENCES, dtype=jnp.int32)[:, None]
    cutoff = 250 + 500 * sequence_ids // max(BATCH_SEQUENCES - 1, 1)
    picks = jax.random.randint(key, (BATCH_SEQUENCES, SEQUENCE_TOKENS), 0, 1000, dtype=jnp.int32)
    counted = (picks < cutoff).astype(jnp.int32)
    first_row = jnp.arange(SEQUENCE_TOKENS, dtype=jnp.int32)[None, :] == 0
    return jnp.where(first_row, 1, counted).astype(jnp.int32)


def level_of(own_key, shape, cuts, smallest, top_value):
    level, own = 1.0, jax.random.fold_in(own_key, 6)
    for axis_at, shards_of in cuts:
        draws = jnp.exp(jax.random.uniform(jax.random.fold_in(own, axis_at), (shards_of,), jnp.float32, smallest / len(cuts), top_value / len(cuts)))
        level = level * jnp.repeat(draws, shape[axis_at] // shards_of).reshape([-1 if axis == axis_at else 1 for axis in range(len(shape))])
    return level


def profile(number_of, total, bound, lean):
    loads = [(1 << 20) // math.isqrt(grade ** lean) + 1 for grade in range(2, number_of + 1)]
    rest, given = total - bound - (number_of - 1), [1] * (number_of - 1)
    while rest > 0:
        free = [i for i in range(number_of - 1) if given[i] < bound]
        whole, remaining = sum([loads[i] for i in free]), rest
        for i in free:
            more = min(bound - given[i], max(1, remaining * loads[i] // whole), rest)
            given[i] = given[i] + more
            rest = rest - more
    return np.array([bound] + given)


def uneven_parts(own_key, count, total, limit, slope):
    if count == 2:
        one = jax.random.randint(own_key, (), max(1, total - limit), min(limit, total - 1) + 1)
        return jnp.stack([one, total - one])
    lengths = jnp.asarray(profile(count, total, limit, slope), jnp.int32)
    twos = (count - 1) // 2
    giver, taker = lengths[1:1 + 2 * twos:2], lengths[2:2 + 2 * twos:2]
    margin = jnp.minimum(giver - 1, limit - taker)
    moved = jax.random.randint(jax.random.fold_in(own_key, 1), (twos,), 0, 1 << 20) % (margin + 1)
    lengths = lengths.at[1:1 + 2 * twos:2].set(giver - moved).at[2:2 + 2 * twos:2].set(taker + moved)
    return lengths[jax.random.permutation(jax.random.fold_in(own_key, 2), count)]


def gaussian(stream_key, shape, scale, bound, pieces=(), held_as=jnp.bfloat16):
    array = scale * jax.random.normal(stream_key, shape, jnp.float32)
    if pieces:
        array = array * level_of(stream_key, shape, pieces, -0.22, 0.18)
    return jnp.clip(array, -bound, bound).astype(held_as)


def setup_inputs(seed: int = 0) -> dict:
    arg_keys = jax.random.split(jax.random.key(seed), 7)
    return {
        "queries": draw_queries(jax.random.fold_in(arg_keys[6], 71), 0),
        "keys": draw_keys(jax.random.fold_in(arg_keys[6], 71), 0),
        "values": gaussian(arg_keys[2], (BATCH_SEQUENCES, SEQUENCE_TOKENS, KEY_VALUE_HEADS * HEAD_SIZE), 1.0, 6.0, ((0, 8), (1, 4))),
        "cotangent": gaussian(arg_keys[3], (BATCH_SEQUENCES, SEQUENCE_TOKENS, QUERY_HEADS * HEAD_SIZE), 1.0, 6.0, ((0, 8), (1, 4))),
        "live": draw_live(jax.random.fold_in(arg_keys[6], 71), 0),
        "docs": jax.vmap(lambda own: jnp.searchsorted(jnp.cumsum(uneven_parts(own, DOCS, SEQUENCE_TOKENS, SEQUENCE_TOKENS // 2, 1)), jnp.arange(SEQUENCE_TOKENS), side="right"))(jax.random.split(arg_keys[5], BATCH_SEQUENCES)).reshape((BATCH_SEQUENCES, SEQUENCE_TOKENS)).astype(jnp.int32),
    }


masked_fill = -1e+30

def folded_positions():
    half_rows = TOK_DEV // 2
    offsets = jnp.arange(SEQUENCE_TOKENS, dtype=jnp.int32)
    slot_index = offsets // half_rows
    device = slot_index // 2
    piece_id = jnp.where(slot_index % 2 == 0, device, 2 * N_CTX - 1 - device)
    return piece_id * half_rows + offsets % half_rows

def one_head(query_head, grad_head, key_natural, value_natural, docs):
    score_scale = 1.0 / math.sqrt(HEAD_SIZE)
    half_rows = TOK_DEV // 2
    outs_list, rows_list = ([], [])
    key_total = jnp.zeros((SEQUENCE_TOKENS, HEAD_SIZE), query_head.dtype)
    value_total = jnp.zeros((SEQUENCE_TOKENS, HEAD_SIZE), query_head.dtype)
    for block in range(N_CTX):
        key_block = jnp.zeros((SEQUENCE_TOKENS, HEAD_SIZE), query_head.dtype)
        value_block = jnp.zeros((SEQUENCE_TOKENS, HEAD_SIZE), query_head.dtype)
        for side in range(2):
            piece_id = block if side == 0 else 2 * N_CTX - 1 - block
            row_start = block * TOK_DEV + side * half_rows
            span = (piece_id + 1) * half_rows
            query_part = query_head[row_start:row_start + half_rows]
            grad_part = grad_head[row_start:row_start + half_rows]
            key_part = key_natural[:span]
            value_part = value_natural[:span]
            query_pos = piece_id * half_rows + jnp.arange(half_rows, dtype=jnp.int32)
            key_pos = jnp.arange(span, dtype=jnp.int32)
            query_doc = docs[piece_id * half_rows:(piece_id + 1) * half_rows]
            allowed = (query_doc[:, None] == docs[:span][None, :]) & (key_pos[None, :] <= query_pos[:, None])
            scores = jnp.einsum('qjd,kd->jqk', query_part, key_part) * score_scale
            masked = jnp.where(allowed, scores, masked_fill)
            row_peak = lax.optimization_barrier(jnp.max(masked, axis=-1, keepdims=True))
            log_total = row_peak + jnp.log(lax.optimization_barrier(jnp.sum(jnp.exp(masked - row_peak), axis=-1, keepdims=True)))
            weights = jnp.where(allowed, jnp.exp(masked - log_total), 0.0)
            rounded = weights.astype(jnp.bfloat16).astype(query_head.dtype)
            attended = jnp.einsum('jqk,kd->qjd', rounded, value_part).astype(jnp.bfloat16)
            delta = jnp.transpose(lax.optimization_barrier(jnp.sum(grad_part * attended.astype(query_head.dtype), axis=-1)))[:, :, None]
            pushes = jnp.einsum('qjd,kd->jqk', grad_part, value_part)
            slopes = (weights * (pushes - delta) * score_scale).astype(jnp.bfloat16).astype(query_head.dtype)
            grad_rows = jnp.einsum('jqk,kd->qjd', slopes, key_part).astype(jnp.bfloat16)
            key_term = jnp.einsum('jqk,qjd->kd', slopes, query_part)
            value_term = jnp.einsum('jqk,qjd->kd', rounded, grad_part)
            key_block = key_block.at[:span].add(key_term)
            value_block = value_block.at[:span].add(value_term)
            outs_list.append(attended)
            rows_list.append(grad_rows)
        key_total = key_total + lax.optimization_barrier(key_block.astype(jnp.bfloat16)).astype(query_head.dtype)
        value_total = value_total + lax.optimization_barrier(value_block.astype(jnp.bfloat16)).astype(query_head.dtype)
    return (jnp.concatenate(outs_list, axis=0), jnp.concatenate(rows_list, axis=0), key_total.astype(jnp.bfloat16), value_total.astype(jnp.bfloat16))

def one_sequence(queries, keys, values, cotangent, live, docs, loss_ratio):
    query_group_width = QUERY_HEADS // KEY_VALUE_HEADS
    positions = folded_positions()
    inverse = jnp.zeros((SEQUENCE_TOKENS,), jnp.int32).at[positions].set(jnp.arange(SEQUENCE_TOKENS, dtype=jnp.int32))
    work_type = loss_ratio.dtype
    output_gradient = (cotangent.astype(work_type) * live.astype(work_type)[:, None] * loss_ratio).astype(jnp.bfloat16)
    query_heads = jnp.transpose(queries.reshape(SEQUENCE_TOKENS, KEY_VALUE_HEADS, query_group_width, HEAD_SIZE).astype(work_type), (1, 0, 2, 3))
    grad_heads = jnp.transpose(output_gradient.reshape(SEQUENCE_TOKENS, KEY_VALUE_HEADS, query_group_width, HEAD_SIZE).astype(work_type), (1, 0, 2, 3))
    key_heads = jnp.transpose(jnp.take(keys, inverse, axis=0).reshape(SEQUENCE_TOKENS, KEY_VALUE_HEADS, HEAD_SIZE).astype(work_type), (1, 0, 2))
    value_heads = jnp.transpose(jnp.take(values, inverse, axis=0).reshape(SEQUENCE_TOKENS, KEY_VALUE_HEADS, HEAD_SIZE).astype(work_type), (1, 0, 2))

    def per_head(operands):
        return one_head(operands[0], operands[1], operands[2], operands[3], docs)
    attended, grad_rows, key_sum, value_sum = lax.map(per_head, (query_heads, grad_heads, key_heads, value_heads))
    attended_all = jnp.transpose(attended, (1, 0, 2, 3)).reshape(SEQUENCE_TOKENS, QUERY_HEADS * HEAD_SIZE)
    grad_queries = jnp.transpose(grad_rows, (1, 0, 2, 3)).reshape(SEQUENCE_TOKENS, QUERY_HEADS * HEAD_SIZE)
    key_gradient = jnp.take(jnp.transpose(key_sum, (1, 0, 2)), positions, axis=0).reshape(SEQUENCE_TOKENS, KEY_VALUE_HEADS * HEAD_SIZE)
    value_gradient = jnp.take(jnp.transpose(value_sum, (1, 0, 2)), positions, axis=0).reshape(SEQUENCE_TOKENS, KEY_VALUE_HEADS * HEAD_SIZE)
    return (attended_all, grad_queries, key_gradient, value_gradient)

def reference(queries, keys, values, cotangent, live, docs):
    live_count = jnp.sum(live).astype(jnp.float32)
    loss_ratio = float(BATCH_SEQUENCES * SEQUENCE_TOKENS) / live_count

    def per_sequence(operands):
        return one_sequence(operands[0], operands[1], operands[2], operands[3], operands[4], operands[5], loss_ratio)
    return lax.map(per_sequence, (queries, keys, values, cotangent, live, docs))
```

```python
import functools
import math

import jax
import jax.numpy as jnp
from jax import lax
from jax.experimental import pallas as pl
from jax.experimental.pallas import tpu as pltpu
from jax.sharding import PartitionSpec as P

HEAD_SIZE = 128
MESH = pl.DeviceIdType.MESH
masked_fill = -1e30
f32, bf16 = jnp.float32, jnp.bfloat16


def matmul(a, b):
    return jnp.dot(a, b, preferred_element_type=f32)


def matmul_nt(a, b):
    return lax.dot_general(a, b, (((1,), (1,)), ((), ())), preferred_element_type=f32)


def kernel(
    n, depth, q_hbm, k_hbm, v_hbm, c_hbm, live_hbm, docs_ref,
    att_hbm, gq_hbm, kg_ref, vg_ref,
    q, cot, kv, tx, rx, att, gq, acc_k, acc_v, bias_a, bias_b, doc_col, scale_rows, live1, live2,
    in_sem, own_sem, ks, kr, gs, gr, l1s, l1r, l2s, l2r, out_sem,
):
    rows = q.shape[0]
    half_rows = rows // 2
    groups = kv.shape[0]
    width = q.shape[1] // groups
    heads = width // HEAD_SIZE
    lanes = heads * half_rows
    chunks = 2 * n
    me, my_dp = lax.axis_index("ctx"), lax.axis_index("dp")
    score_scale = 1.0 / math.sqrt(HEAD_SIZE)

    def chunk_of(device, half):
        return device if half == 0 else chunks - 1 - device

    def needs(device, chunk):
        first = chunk <= device
        second = (chunk >= n - 1 - device) & (chunk <= chunks - 1 - device)
        return first | second

    def ahead(k):
        return lax.rem(me + k, n)

    def behind(k):
        return lax.rem(me + n - k, n)

    def dp_ahead(k):
        return lax.rem(my_dp + k, depth)

    barrier = pltpu.get_barrier_semaphore()
    for k in range(1, n):
        pl.semaphore_signal(barrier, inc=1, device_id=(my_dp, ahead(k)), device_id_type=MESH)
    for k in range(1, depth):
        pl.semaphore_signal(barrier, inc=1, device_id=(dp_ahead(k), me), device_id_type=MESH)

    def own_copy(g, half, which):
        source = k_hbm if which == 0 else v_hbm
        return pltpu.make_async_copy(
            source.at[pl.ds(half * half_rows, half_rows), pl.ds(g * HEAD_SIZE, HEAD_SIZE)],
            kv.at[g, chunk_of(me, half), which],
            own_sem.at[g, half, which],
        )

    live_copy = pltpu.make_async_copy(live_hbm, live1.at[0], in_sem.at[2])
    live_copy.start()
    for g in range(groups):
        for half in range(2):
            for which in range(2):
                own_copy(g, half, which).start()
    q_copy = pltpu.make_async_copy(q_hbm, q, in_sem.at[0])
    c_copy = pltpu.make_async_copy(c_hbm, cot, in_sem.at[1])
    q_copy.start()
    c_copy.start()

    def clear(chunk, carry):
        @pl.when(jnp.logical_not(needs(me, chunk)))
        def _():
            for g in range(groups):
                kv[g, chunk] = jnp.zeros(kv.shape[2:], bf16)

        return carry

    lax.fori_loop(0, chunks, clear, 0)

    for b in range(doc_col.shape[0] // HEAD_SIZE):
        piece = docs_ref[0:1, b * HEAD_SIZE:(b + 1) * HEAD_SIZE].astype(f32)
        doc_col[b * HEAD_SIZE:(b + 1) * HEAD_SIZE, :] = jnp.transpose(
            jnp.broadcast_to(piece, (HEAD_SIZE, HEAD_SIZE))
        )
    first_b = ((n - 1 - me) // 2) * 2

    def build(bias, key_chunk, query_chunk):
        size = bias.shape[0]
        start = key_chunk * half_rows
        key_doc = doc_col[pl.ds(pl.multiple_of(start, half_rows), size), 0:1]
        key_pos = start + lax.broadcasted_iota(jnp.int32, (size, lanes), 0)
        query_pos = query_chunk * half_rows + lax.rem(
            lax.broadcasted_iota(jnp.int32, (size, lanes), 1), half_rows
        )
        query_doc = jnp.sum(
            jnp.where(key_pos == query_pos, key_doc, 0.0), axis=0, keepdims=True
        )
        allowed = (key_doc == query_doc) & (key_pos <= query_pos)
        bias[...] = jnp.where(allowed, 0.0, masked_fill)

    build(bias_a, 0, chunk_of(me, 0))
    build(bias_b, first_b, chunk_of(me, 1))

    live_copy.wait()
    for g in range(groups):
        for half in range(2):
            for which in range(2):
                own_copy(g, half, which).wait()
    pl.semaphore_wait(barrier, n - 1 + depth - 1)

    def live1_copy(k):
        return pltpu.make_async_remote_copy(
            src_ref=live1.at[0], dst_ref=live1.at[k], send_sem=l1s.at[k], recv_sem=l1r.at[k],
            device_id=(my_dp, ahead(k)), device_id_type=MESH,
        )

    def live2_copy(k):
        return pltpu.make_async_remote_copy(
            src_ref=live2.at[0], dst_ref=live2.at[k], send_sem=l2s.at[k], recv_sem=l2r.at[k],
            device_id=(dp_ahead(k), me), device_id_type=MESH,
        )

    def gather_copy(g, k, half, chunk):
        return pltpu.make_async_remote_copy(
            src_ref=kv.at[g, chunk], dst_ref=kv.at[g, chunk],
            send_sem=ks.at[g, k, half], recv_sem=kr.at[g, k, half],
            device_id=(my_dp, ahead(k)), device_id_type=MESH,
        )

    def scatter_copy(g, k, half, chunk):
        return pltpu.make_async_remote_copy(
            src_ref=tx.at[g, chunk], dst_ref=rx.at[g, k, half],
            send_sem=gs.at[g, k, half], recv_sem=gr.at[g, k, half],
            device_id=(my_dp, ahead(k)), device_id_type=MESH,
        )

    for k in range(1, n):
        live1_copy(k).start()

    def send_keys(g, carry):
        for k in range(1, n):
            for half in range(2):
                chunk = chunk_of(me, half)

                @pl.when(needs(ahead(k), chunk))
                def _(k=k, half=half, chunk=chunk):
                    gather_copy(g, k, half, chunk).start()

        return carry

    lax.fori_loop(0, groups, send_keys, 0)

    for k in range(1, n):
        live1_copy(k).wait()
    live2[0] = jnp.sum(live1[...], axis=0)
    for k in range(1, depth):
        live2_copy(k).start()
    q_copy.wait()
    c_copy.wait()

    def att_copy(g):
        return pltpu.make_async_copy(
            att.at[g], att_hbm.at[:, pl.ds(pl.multiple_of(g * width, width), width)],
            out_sem.at[0, g],
        )

    def gq_copy(g):
        return pltpu.make_async_copy(
            gq.at[g], gq_hbm.at[:, pl.ds(pl.multiple_of(g * width, width), width)],
            out_sem.at[1, g],
        )

    def stacked(source, g, half):
        return [
            source[
                half * half_rows:(half + 1) * half_rows,
                pl.ds(pl.multiple_of(g * width + j * HEAD_SIZE, HEAD_SIZE), HEAD_SIZE),
            ]
            for j in range(heads)
        ]

    def group_step(g, carry):
        for k in range(1, n):
            for half in range(2):
                chunk = chunk_of(behind(k), half)

                @pl.when(needs(me, chunk))
                def _(k=k, half=half, chunk=chunk):
                    gather_copy(g, k, half, chunk).wait_recv()

        @pl.when(g == 0)
        def _():
            for k in range(1, depth):
                live2_copy(k).wait()
            count = jnp.sum(
                jnp.sum(live2[...].astype(f32), axis=0), axis=1, keepdims=True
            )
            ratio = float(depth * n * rows) / count
            live_row = live1[0].astype(f32)
            scale_rows[...] = (
                jnp.transpose(jnp.broadcast_to(live_row, (HEAD_SIZE, rows))) * ratio
            )

        for half in range(2):
            bias = bias_a if half == 0 else bias_b
            size = bias.shape[0]
            count = size // half_rows
            window = pl.ds(0 if half == 0 else first_b, count)
            low, high = half * half_rows, (half + 1) * half_rows
            keys = kv[g, window, 0].reshape(size, HEAD_SIZE)
            values = kv[g, window, 1].reshape(size, HEAD_SIZE)
            queries = jnp.concatenate(stacked(q, g, half), axis=0)
            grads = jnp.concatenate(
                [(c.astype(f32) * scale_rows[low:high, :]).astype(bf16)
                 for c in stacked(cot, g, half)],
                axis=0,
            )
            scores = matmul_nt(keys, queries) * score_scale + bias[...]
            peak = jnp.max(scores, axis=0, keepdims=True)
            mass = jnp.exp(scores - peak)
            total = jnp.sum(mass, axis=0, keepdims=True)
            weights = mass * (1.0 / total)
            rounded = weights.astype(bf16)
            out_t = matmul(jnp.transpose(values), rounded).astype(bf16).astype(f32)
            delta = jnp.sum(jnp.transpose(grads.astype(f32)) * out_t, axis=0, keepdims=True)
            out = jnp.transpose(out_t).astype(bf16)
            pushes = matmul_nt(values, grads)
            slopes = (weights * (pushes - delta) * score_scale).astype(bf16)
            rows_t = matmul(jnp.transpose(keys), slopes)
            grad_rows = jnp.transpose(rows_t).astype(bf16)
            for j in range(heads):
                columns = pl.ds(j * HEAD_SIZE, HEAD_SIZE)
                att[g, low:high, columns] = out[j * half_rows:(j + 1) * half_rows, :]
                gq[g, low:high, columns] = grad_rows[j * half_rows:(j + 1) * half_rows, :]
            key_part = matmul(slopes, queries).reshape(count, half_rows, HEAD_SIZE)
            value_part = matmul(rounded, grads).reshape(count, half_rows, HEAD_SIZE)
            if half == 0:
                rest = jnp.zeros((chunks - count, half_rows, HEAD_SIZE), f32)
                acc_k[0:count] = key_part
                acc_v[0:count] = value_part
                acc_k[count:] = rest
                acc_v[count:] = rest
            else:
                acc_k[window] += key_part
                acc_v[window] += value_part
        att_copy(g).start()
        gq_copy(g).start()
        tx[g, :, 0] = acc_k[...].astype(bf16)
        tx[g, :, 1] = acc_v[...].astype(bf16)
        for k in range(1, n):
            for half in range(2):
                chunk = chunk_of(ahead(k), half)

                @pl.when(needs(me, chunk))
                def _(k=k, half=half, chunk=chunk):
                    scatter_copy(g, k, half, chunk).start()

        return carry

    lax.fori_loop(0, groups, group_step, 0)

    def reduce_step(g, carry):
        columns = pl.ds(pl.multiple_of(g * HEAD_SIZE, HEAD_SIZE), HEAD_SIZE)
        for half in range(2):
            mine = chunk_of(me, half)
            low, high = half * half_rows, (half + 1) * half_rows
            acc_k[0] = tx[g, mine, 0].astype(f32)
            acc_v[0] = tx[g, mine, 1].astype(f32)
            for k in range(1, n):

                @pl.when(needs(behind(k), mine))
                def _(k=k, half=half):
                    scatter_copy(g, k, half, mine).wait_recv()
                    acc_k[0] += rx[g, k, half, 0].astype(f32)
                    acc_v[0] += rx[g, k, half, 1].astype(f32)

            kg_ref[low:high, columns] = acc_k[0].astype(bf16)
            vg_ref[low:high, columns] = acc_v[0].astype(bf16)
        return carry

    lax.fori_loop(0, groups, reduce_step, 0)

    def drain(g, carry):
        for k in range(1, n):
            for half in range(2):
                mine, theirs = chunk_of(me, half), chunk_of(ahead(k), half)

                @pl.when(needs(ahead(k), mine))
                def _(k=k, half=half):
                    gather_copy(g, k, half, mine).wait_send()

                @pl.when(needs(me, theirs))
                def _(k=k, half=half):
                    scatter_copy(g, k, half, theirs).wait_send()

        att_copy(g).wait()
        gq_copy(g).wait()
        return carry

    lax.fori_loop(0, groups, drain, 0)


def on_device(n, depth, queries, keys, values, cotangent, live, docs):
    rows, q_width = queries.shape[1:]
    kv_width = keys.shape[2]
    groups = kv_width // HEAD_SIZE
    width = q_width // groups
    heads = width // HEAD_SIZE
    half_rows = rows // 2
    chunks = 2 * n
    lanes = heads * half_rows
    anywhere = pl.BlockSpec(memory_space=pl.ANY)
    vmem = pl.BlockSpec(memory_space=pltpu.VMEM)
    dma = pltpu.SemaphoreType.DMA
    block = (2, half_rows, HEAD_SIZE)
    attended, grad_queries, key_gradient, value_gradient = pl.pallas_call(
        functools.partial(kernel, n, depth),
        out_shape=(
            jax.ShapeDtypeStruct((rows, q_width), bf16),
            jax.ShapeDtypeStruct((rows, q_width), bf16),
            jax.ShapeDtypeStruct((rows, kv_width), bf16),
            jax.ShapeDtypeStruct((rows, kv_width), bf16),
        ),
        in_specs=[anywhere] * 5 + [vmem],
        out_specs=(anywhere, anywhere, vmem, vmem),
        scratch_shapes=[
            pltpu.VMEM((rows, q_width), bf16),
            pltpu.VMEM((rows, q_width), bf16),
            pltpu.VMEM((groups, chunks) + block, bf16),
            pltpu.VMEM((groups, chunks) + block, bf16),
            pltpu.VMEM((groups, n, 2) + block, bf16),
            pltpu.VMEM((groups, rows, width), bf16),
            pltpu.VMEM((groups, rows, width), bf16),
            pltpu.VMEM((chunks, half_rows, HEAD_SIZE), f32),
            pltpu.VMEM((chunks, half_rows, HEAD_SIZE), f32),
            pltpu.VMEM((n * half_rows, lanes), f32),
            pltpu.VMEM(((n + 2) * half_rows, lanes), f32),
            pltpu.VMEM((n * rows, HEAD_SIZE), f32),
            pltpu.VMEM((rows, HEAD_SIZE), f32),
            pltpu.VMEM((n, 1, rows), jnp.int32),
            pltpu.VMEM((depth, 1, rows), jnp.int32),
            dma((3,)),
            dma((groups, 2, 2)),
            dma((groups, n, 2)),
            dma((groups, n, 2)),
            dma((groups, n, 2)),
            dma((groups, n, 2)),
            dma((n,)),
            dma((n,)),
            dma((depth,)),
            dma((depth,)),
            dma((2, groups)),
        ],
        compiler_params=pltpu.CompilerParams(
            collective_id=0, has_side_effects=True, vmem_limit_bytes=60 * 1024 * 1024
        ),
    )(queries[0], keys[0], values[0], cotangent[0], live, docs)
    return attended[None], grad_queries[None], key_gradient[None], value_gradient[None]


def solution(mesh):
    wide = P("dp", "ctx", None)
    return jax.shard_map(
        functools.partial(on_device, mesh.shape["ctx"], mesh.shape["dp"]),
        mesh=mesh,
        in_specs=(wide, wide, wide, wide, P("dp", "ctx"), P("dp", None)),
        out_specs=(wide, wide, wide, wide),
        check_vma=False,
    )
```

```python
import functools
import math

import jax
import jax.numpy as jnp
from jax import lax
from jax.experimental import pallas as pl
from jax.experimental.pallas import tpu as pltpu
from jax.sharding import PartitionSpec as P

HEAD_SIZE = 128
MESH = pl.DeviceIdType.MESH
masked_fill = -1e30
f32, bf16 = jnp.float32, jnp.bfloat16


def matmul(a, b):
    return jnp.dot(a, b, preferred_element_type=f32)


def matmul_nt(a, b):
    return lax.dot_general(a, b, (((1,), (1,)), ((), ())), preferred_element_type=f32)


def kernel(
    n, depth, q_hbm, k_hbm, v_hbm, c_hbm, live_hbm, docs_ref,
    att, gq, kg_ref, vg_ref,
    q, cot, kv, tx, rx, gq32, acc_k, acc_v, bias_a, bias_b, doc_col, live_rows, live1, live2, live3,
    in_sem, own_sem, ks, kr, gs, gr, l1s, l1r, l2s, l2r,
):
    rows = q.shape[0]
    half_rows = rows // 2
    groups = kv.shape[0]
    width = q.shape[1] // groups
    heads = width // HEAD_SIZE
    lanes = heads * half_rows
    chunks = 2 * n
    me, my_dp = lax.axis_index("ctx"), lax.axis_index("dp")
    score_scale = 1.0 / math.sqrt(HEAD_SIZE)

    def chunk_of(device, half):
        return device if half == 0 else chunks - 1 - device

    def needs(device, chunk):
        first = chunk <= device
        second = (chunk >= n - 1 - device) & (chunk <= chunks - 1 - device)
        return first | second

    def ahead(k):
        return lax.rem(me + k, n)

    def behind(k):
        return lax.rem(me + n - k, n)

    stages = depth.bit_length() - 1

    def dp_partner(stage):
        step = 1 << stage
        upper = lax.rem(my_dp // step, 2)
        return my_dp + step - 2 * step * upper

    barrier = pltpu.get_barrier_semaphore()
    for k in range(1, n):
        pl.semaphore_signal(barrier, inc=1, device_id=(my_dp, ahead(k)), device_id_type=MESH)
    for stage in range(stages):
        pl.semaphore_signal(
            barrier, inc=1, device_id=(dp_partner(stage), me), device_id_type=MESH
        )

    def own_copy(g, half, which):
        source = k_hbm if which == 0 else v_hbm
        return pltpu.make_async_copy(
            source.at[pl.ds(half * half_rows, half_rows), pl.ds(g * HEAD_SIZE, HEAD_SIZE)],
            kv.at[g, chunk_of(me, half), which],
            own_sem.at[g, half, which],
        )

    live_copy = pltpu.make_async_copy(live_hbm, live1.at[0], in_sem.at[2])
    live_copy.start()
    for g in range(groups):
        for half in range(2):
            for which in range(2):
                own_copy(g, half, which).start()
    q_copy = pltpu.make_async_copy(q_hbm, q, in_sem.at[0])
    c_copy = pltpu.make_async_copy(c_hbm, cot, in_sem.at[1])
    q_copy.start()
    c_copy.start()

    def clear(chunk, carry):
        @pl.when(jnp.logical_not(needs(me, chunk)))
        def _():
            for g in range(groups):
                kv[g, chunk] = jnp.zeros(kv.shape[2:], bf16)

        return carry

    lax.fori_loop(0, chunks, clear, 0)

    for b in range(doc_col.shape[0] // HEAD_SIZE):
        piece = docs_ref[0:1, b * HEAD_SIZE:(b + 1) * HEAD_SIZE].astype(f32)
        doc_col[b * HEAD_SIZE:(b + 1) * HEAD_SIZE, :] = jnp.transpose(
            jnp.broadcast_to(piece, (HEAD_SIZE, HEAD_SIZE))
        )
    first_b = ((n - 1 - me) // 2) * 2

    def build(bias, key_chunk, query_chunk):
        size = bias.shape[0]
        start = key_chunk * half_rows
        key_doc = doc_col[pl.ds(pl.multiple_of(start, half_rows), size), 0:1]
        key_pos = start + lax.broadcasted_iota(jnp.int32, (size, lanes), 0)
        query_pos = query_chunk * half_rows + lax.rem(
            lax.broadcasted_iota(jnp.int32, (size, lanes), 1), half_rows
        )
        query_doc = jnp.sum(
            jnp.where(key_pos == query_pos, key_doc, 0.0), axis=0, keepdims=True
        )
        allowed = (key_doc == query_doc) & (key_pos <= query_pos)
        bias[...] = jnp.where(allowed, 0.0, masked_fill)

    build(bias_a, 0, chunk_of(me, 0))
    build(bias_b, first_b, chunk_of(me, 1))

    live_copy.wait()
    for g in range(groups):
        for half in range(2):
            for which in range(2):
                own_copy(g, half, which).wait()
    pl.semaphore_wait(barrier, n - 1 + stages)

    def live1_copy(k):
        return pltpu.make_async_remote_copy(
            src_ref=live1.at[0], dst_ref=live1.at[k], send_sem=l1s.at[k], recv_sem=l1r.at[k],
            device_id=(my_dp, ahead(k)), device_id_type=MESH,
        )

    def live2_copy(stage):
        return pltpu.make_async_remote_copy(
            src_ref=live2.at[stage], dst_ref=live3.at[stage],
            send_sem=l2s.at[stage], recv_sem=l2r.at[stage],
            device_id=(dp_partner(stage), me), device_id_type=MESH,
        )

    def live_stage(stage):
        if stage == 0:
            for k in range(1, n):
                live1_copy(k).wait()
            live2[0] = jnp.sum(live1[...], axis=0)
        else:
            live2_copy(stage - 1).wait()
            live2[stage] = live2[stage - 1] + live3[stage - 1]
        if stage < stages:
            live2_copy(stage).start()

    def gather_copy(g, k, half, chunk):
        return pltpu.make_async_remote_copy(
            src_ref=kv.at[g, chunk], dst_ref=kv.at[g, chunk],
            send_sem=ks.at[g, k, half], recv_sem=kr.at[g, k, half],
            device_id=(my_dp, ahead(k)), device_id_type=MESH,
        )

    def scatter_copy(g, k, half, chunk):
        return pltpu.make_async_remote_copy(
            src_ref=tx.at[g, chunk], dst_ref=rx.at[g, k, half],
            send_sem=gs.at[g, k, half], recv_sem=gr.at[g, k, half],
            device_id=(my_dp, ahead(k)), device_id_type=MESH,
        )

    for k in range(1, n):
        live1_copy(k).start()

    def send_keys(g, carry):
        for k in range(1, n):
            for half in range(2):
                chunk = chunk_of(me, half)

                @pl.when(needs(ahead(k), chunk))
                def _(k=k, half=half, chunk=chunk):
                    gather_copy(g, k, half, chunk).start()

        return carry

    lax.fori_loop(0, groups, send_keys, 0)

    live_rows[...] = jnp.transpose(
        jnp.broadcast_to(live1[0].astype(f32), (HEAD_SIZE, rows))
    )
    live_stage(0)
    q_copy.wait()
    c_copy.wait()

    def stacked(source, g, half):
        return [
            source[
                half * half_rows:(half + 1) * half_rows,
                pl.ds(pl.multiple_of(g * width + j * HEAD_SIZE, HEAD_SIZE), HEAD_SIZE),
            ]
            for j in range(heads)
        ]

    def group_step(g, carry):
        for k in range(1, n):
            for half in range(2):
                chunk = chunk_of(behind(k), half)

                @pl.when(needs(me, chunk))
                def _(k=k, half=half, chunk=chunk):
                    gather_copy(g, k, half, chunk).wait_recv()

        for half in range(2):
            bias = bias_a if half == 0 else bias_b
            size = bias.shape[0]
            count = size // half_rows
            window = pl.ds(0 if half == 0 else first_b, count)
            low, high = half * half_rows, (half + 1) * half_rows
            keys = kv[g, window, 0].reshape(size, HEAD_SIZE)
            values = kv[g, window, 1].reshape(size, HEAD_SIZE)
            queries = jnp.concatenate(stacked(q, g, half), axis=0)
            grads = jnp.concatenate(
                [(c.astype(f32) * live_rows[low:high, :]).astype(bf16)
                 for c in stacked(cot, g, half)],
                axis=0,
            )
            scores = matmul_nt(keys, queries) * score_scale + bias[...]
            peak = jnp.max(scores, axis=0, keepdims=True)
            mass = jnp.exp(scores - peak)
            total = jnp.sum(mass, axis=0, keepdims=True)
            weights = mass * (1.0 / total)
            rounded = weights.astype(bf16)
            out_t = matmul(jnp.transpose(values), rounded).astype(bf16).astype(f32)
            delta = jnp.sum(jnp.transpose(grads.astype(f32)) * out_t, axis=0, keepdims=True)
            out = jnp.transpose(out_t).astype(bf16)
            pushes = matmul_nt(values, grads)
            slopes = (weights * (pushes - delta) * score_scale).astype(bf16)
            rows_t = matmul(jnp.transpose(keys), slopes)
            grad_rows = jnp.transpose(rows_t)
            for j in range(heads):
                columns = pl.ds(j * HEAD_SIZE, HEAD_SIZE)
                wide = pl.ds(pl.multiple_of(g * width + j * HEAD_SIZE, HEAD_SIZE), HEAD_SIZE)
                att[low:high, wide] = out[j * half_rows:(j + 1) * half_rows, :]
                gq32[g, low:high, columns] = grad_rows[j * half_rows:(j + 1) * half_rows, :]
            key_part = matmul(slopes, queries).reshape(count, half_rows, HEAD_SIZE)
            value_part = matmul(rounded, grads).reshape(count, half_rows, HEAD_SIZE)
            if half == 0:
                rest = jnp.zeros((chunks - count, half_rows, HEAD_SIZE), f32)
                acc_k[0:count] = key_part
                acc_v[0:count] = value_part
                acc_k[count:] = rest
                acc_v[count:] = rest
            else:
                acc_k[window] += key_part
                acc_v[window] += value_part
        tx[g, :, 0] = acc_k[...].astype(bf16)
        tx[g, :, 1] = acc_v[...].astype(bf16)
        for k in range(1, n):
            for half in range(2):
                chunk = chunk_of(ahead(k), half)

                @pl.when(needs(me, chunk))
                def _(k=k, half=half, chunk=chunk):
                    scatter_copy(g, k, half, chunk).start()

        for stage in range(1, stages + 1):

            @pl.when(g == min(stage - 1, groups - 1))
            def _(stage=stage):
                live_stage(stage)

        return carry

    lax.fori_loop(0, groups, group_step, 0)

    count = jnp.sum(live2[stages].astype(f32), axis=1, keepdims=True)
    ratio = float(depth * n * rows) / count

    def scale_step(g, carry):
        wide = pl.ds(pl.multiple_of(g * width, width), width)
        gq[:, wide] = (gq32[g] * ratio).astype(bf16)
        return carry

    lax.fori_loop(0, groups, scale_step, 0)

    def reduce_step(g, carry):
        columns = pl.ds(pl.multiple_of(g * HEAD_SIZE, HEAD_SIZE), HEAD_SIZE)
        for half in range(2):
            mine = chunk_of(me, half)
            low, high = half * half_rows, (half + 1) * half_rows
            acc_k[0] = tx[g, mine, 0].astype(f32)
            acc_v[0] = tx[g, mine, 1].astype(f32)
            for k in range(1, n):

                @pl.when(needs(behind(k), mine))
                def _(k=k, half=half):
                    scatter_copy(g, k, half, mine).wait_recv()
                    acc_k[0] += rx[g, k, half, 0].astype(f32)
                    acc_v[0] += rx[g, k, half, 1].astype(f32)

            kg_ref[low:high, columns] = (acc_k[0] * ratio).astype(bf16)
            vg_ref[low:high, columns] = (acc_v[0] * ratio).astype(bf16)
        return carry

    lax.fori_loop(0, groups, reduce_step, 0)

    def drain(g, carry):
        for k in range(1, n):
            for half in range(2):
                mine, theirs = chunk_of(me, half), chunk_of(ahead(k), half)

                @pl.when(needs(ahead(k), mine))
                def _(k=k, half=half):
                    gather_copy(g, k, half, mine).wait_send()

                @pl.when(needs(me, theirs))
                def _(k=k, half=half):
                    scatter_copy(g, k, half, theirs).wait_send()

        return carry

    lax.fori_loop(0, groups, drain, 0)


def store_kernel(*refs):
    sources, targets, sem = refs[:4], refs[4:8], refs[8]
    copies = [
        pltpu.make_async_copy(source, target, sem.at[i])
        for i, (source, target) in enumerate(zip(sources, targets))
    ]
    for copy in copies:
        copy.start()
    for copy in copies:
        copy.wait()


def on_device(n, depth, queries, keys, values, cotangent, live, docs):
    rows, q_width = queries.shape[1:]
    kv_width = keys.shape[2]
    groups = kv_width // HEAD_SIZE
    width = q_width // groups
    heads = width // HEAD_SIZE
    half_rows = rows // 2
    chunks = 2 * n
    lanes = heads * half_rows
    anywhere = pl.BlockSpec(memory_space=pl.ANY)
    vmem = pl.BlockSpec(memory_space=pltpu.VMEM)
    dma = pltpu.SemaphoreType.DMA
    block = (2, half_rows, HEAD_SIZE)
    shapes = ((rows, q_width),) * 2 + ((rows, kv_width),) * 2
    stages = depth.bit_length() - 1
    if depth != 1 << stages:
        raise ValueError("dp size")
    results = pl.pallas_call(
        functools.partial(kernel, n, depth),
        out_shape=tuple(pltpu.VMEM(shape, bf16) for shape in shapes),
        in_specs=[anywhere] * 5 + [vmem],
        out_specs=(vmem,) * 4,
        scratch_shapes=[
            pltpu.VMEM((rows, q_width), bf16),
            pltpu.VMEM((rows, q_width), bf16),
            pltpu.VMEM((groups, chunks) + block, bf16),
            pltpu.VMEM((groups, chunks) + block, bf16),
            pltpu.VMEM((groups, n, 2) + block, bf16),
            pltpu.VMEM((groups, rows, width), f32),
            pltpu.VMEM((chunks, half_rows, HEAD_SIZE), f32),
            pltpu.VMEM((chunks, half_rows, HEAD_SIZE), f32),
            pltpu.VMEM((n * half_rows, lanes), f32),
            pltpu.VMEM(((n + 2) * half_rows, lanes), f32),
            pltpu.VMEM((n * rows, HEAD_SIZE), f32),
            pltpu.VMEM((rows, HEAD_SIZE), f32),
            pltpu.VMEM((n, 1, rows), jnp.int32),
            pltpu.VMEM((stages + 1, 1, rows), jnp.int32),
            pltpu.VMEM((max(stages, 1), 1, rows), jnp.int32),
            dma((3,)),
            dma((groups, 2, 2)),
            dma((groups, n, 2)),
            dma((groups, n, 2)),
            dma((groups, n, 2)),
            dma((groups, n, 2)),
            dma((n,)),
            dma((n,)),
            dma((max(stages, 1),)),
            dma((max(stages, 1),)),
        ],
        compiler_params=pltpu.CompilerParams(
            collective_id=0, has_side_effects=True, vmem_limit_bytes=60 * 1024 * 1024
        ),
    )(queries[0], keys[0], values[0], cotangent[0], live, docs)
    outputs = pl.pallas_call(
        store_kernel,
        out_shape=tuple(jax.ShapeDtypeStruct(shape, bf16) for shape in shapes),
        in_specs=[vmem] * 4,
        out_specs=(anywhere,) * 4,
        scratch_shapes=[dma((4,))],
        compiler_params=pltpu.CompilerParams(vmem_limit_bytes=16 * 1024 * 1024),
    )(*results)
    return tuple(output[None] for output in outputs)


def solution(mesh):
    wide = P("dp", "ctx", None)
    return jax.shard_map(
        functools.partial(on_device, mesh.shape["ctx"], mesh.shape["dp"]),
        mesh=mesh,
        in_specs=(wide, wide, wide, wide, P("dp", "ctx"), P("dp", None)),
        out_specs=(wide, wide, wide, wide),
        check_vma=False,
    )
```

```python
import functools
import math

import jax
import jax.numpy as jnp
from jax import lax
from jax.experimental import pallas as pl
from jax.experimental.pallas import tpu as pltpu
from jax.sharding import PartitionSpec as P

HEAD_SIZE = 128
MESH = pl.DeviceIdType.MESH
masked_fill = -1e30
f32, bf16 = jnp.float32, jnp.bfloat16


def matmul(a, b):
    return jnp.dot(a, b, preferred_element_type=f32)


def matmul_nt(a, b):
    return lax.dot_general(a, b, (((1,), (1,)), ((), ())), preferred_element_type=f32)


def kernel(
    n, depth, q_hbm, k_hbm, v_hbm, c_hbm, live_hbm, docs_ref,
    att, gq, kg_ref, vg_ref,
    q, cot, kv, tx, rx, gq32, acc_k, acc_v, bias_a, bias_b, doc_col, live_rows, live1, live2, live3,
    in_sem, own_sem, ks, kr, gs, gr, l1s, l1r, l2s, l2r,
):
    rows = q.shape[0]
    half_rows = rows // 2
    groups = kv.shape[0]
    width = q.shape[1] // groups
    heads = width // HEAD_SIZE
    lanes = heads * half_rows
    chunks = 2 * n
    me, my_dp = lax.axis_index("ctx"), lax.axis_index("dp")
    score_scale = 1.0 / math.sqrt(HEAD_SIZE)

    def chunk_of(device, half):
        return device if half == 0 else chunks - 1 - device

    def needs(device, chunk):
        first = chunk <= device
        second = (chunk >= n - 1 - device) & (chunk <= chunks - 1 - device)
        return first | second

    def ahead(k):
        return lax.rem(me + k, n)

    def behind(k):
        return lax.rem(me + n - k, n)

    stages = depth.bit_length() - 1

    def dp_partner(stage):
        step = 1 << stage
        upper = lax.rem(my_dp // step, 2)
        return my_dp + step - 2 * step * upper

    barrier = pltpu.get_barrier_semaphore()
    for k in range(1, n):
        pl.semaphore_signal(barrier, inc=1, device_id=(my_dp, ahead(k)), device_id_type=MESH)
    for stage in range(stages):
        pl.semaphore_signal(
            barrier, inc=1, device_id=(dp_partner(stage), me), device_id_type=MESH
        )

    def own_copy(g, half, which):
        source = k_hbm if which == 0 else v_hbm
        return pltpu.make_async_copy(
            source.at[pl.ds(half * half_rows, half_rows), pl.ds(g * HEAD_SIZE, HEAD_SIZE)],
            kv.at[g, chunk_of(me, half), which],
            own_sem.at[g, half, which],
        )

    live_copy = pltpu.make_async_copy(live_hbm, live1.at[0], in_sem.at[2])
    live_copy.start()
    for g in range(groups):
        for half in range(2):
            for which in range(2):
                own_copy(g, half, which).start()
    q_copy = pltpu.make_async_copy(q_hbm, q, in_sem.at[0])
    c_copy = pltpu.make_async_copy(c_hbm, cot, in_sem.at[1])
    q_copy.start()
    c_copy.start()

    def clear(chunk, carry):
        @pl.when(jnp.logical_not(needs(me, chunk)))
        def _():
            for g in range(groups):
                kv[g, chunk] = jnp.zeros(kv.shape[2:], bf16)

        return carry

    lax.fori_loop(0, chunks, clear, 0)

    for b in range(doc_col.shape[0] // HEAD_SIZE):
        piece = docs_ref[0:1, b * HEAD_SIZE:(b + 1) * HEAD_SIZE].astype(f32)
        doc_col[b * HEAD_SIZE:(b + 1) * HEAD_SIZE, :] = jnp.transpose(
            jnp.broadcast_to(piece, (HEAD_SIZE, HEAD_SIZE))
        )
    first_b = ((n - 1 - me) // 2) * 2

    def build(bias, key_chunk, query_chunk):
        size = bias.shape[0]
        start = key_chunk * half_rows
        key_doc = doc_col[pl.ds(pl.multiple_of(start, half_rows), size), 0:1]
        key_pos = start + lax.broadcasted_iota(jnp.int32, (size, lanes), 0)
        query_pos = query_chunk * half_rows + lax.rem(
            lax.broadcasted_iota(jnp.int32, (size, lanes), 1), half_rows
        )
        query_doc = jnp.sum(
            jnp.where(key_pos == query_pos, key_doc, 0.0), axis=0, keepdims=True
        )
        allowed = (key_doc == query_doc) & (key_pos <= query_pos)
        bias[...] = jnp.where(allowed, 0.0, masked_fill)

    build(bias_a, 0, chunk_of(me, 0))
    build(bias_b, first_b, chunk_of(me, 1))

    live_copy.wait()
    for g in range(groups):
        for half in range(2):
            for which in range(2):
                own_copy(g, half, which).wait()
    pl.semaphore_wait(barrier, n - 1 + stages)

    def live1_copy(k):
        return pltpu.make_async_remote_copy(
            src_ref=live1.at[0], dst_ref=live1.at[k], send_sem=l1s.at[k], recv_sem=l1r.at[k],
            device_id=(my_dp, ahead(k)), device_id_type=MESH,
        )

    def live2_copy(stage):
        return pltpu.make_async_remote_copy(
            src_ref=live2.at[stage], dst_ref=live3.at[stage],
            send_sem=l2s.at[stage], recv_sem=l2r.at[stage],
            device_id=(dp_partner(stage), me), device_id_type=MESH,
        )

    def live_stage(stage):
        if stage == 0:
            for k in range(1, n):
                live1_copy(k).wait()
            live2[0] = jnp.sum(live1[...], axis=0)
        else:
            live2_copy(stage - 1).wait()
            live2[stage] = live2[stage - 1] + live3[stage - 1]
        if stage < stages:
            live2_copy(stage).start()

    def gather_copy(g, k, half, chunk):
        return pltpu.make_async_remote_copy(
            src_ref=kv.at[g, chunk], dst_ref=kv.at[g, chunk],
            send_sem=ks.at[g, k, half], recv_sem=kr.at[g, k, half],
            device_id=(my_dp, ahead(k)), device_id_type=MESH,
        )

    def scatter_copy(g, k, half, chunk):
        return pltpu.make_async_remote_copy(
            src_ref=tx.at[g, chunk], dst_ref=rx.at[g, k, half],
            send_sem=gs.at[g, k, half], recv_sem=gr.at[g, k, half],
            device_id=(my_dp, ahead(k)), device_id_type=MESH,
        )

    for k in range(1, n):
        live1_copy(k).start()

    far_first = sorted(range(1, n), key=lambda k: -min(k, n - k))

    def send_keys(g, carry):
        for k in far_first:
            for half in range(2):
                chunk = chunk_of(me, half)

                @pl.when(needs(ahead(k), chunk))
                def _(k=k, half=half, chunk=chunk):
                    gather_copy(g, k, half, chunk).start()

        return carry

    lax.fori_loop(0, groups, send_keys, 0)

    live_rows[...] = jnp.transpose(
        jnp.broadcast_to(live1[0].astype(f32), (HEAD_SIZE, rows))
    )
    live_stage(0)
    q_copy.wait()
    c_copy.wait()

    def stacked(source, g, half):
        return [
            source[
                half * half_rows:(half + 1) * half_rows,
                pl.ds(pl.multiple_of(g * width + j * HEAD_SIZE, HEAD_SIZE), HEAD_SIZE),
            ]
            for j in range(heads)
        ]

    def group_step(g, carry):
        for k in range(1, n):
            for half in range(2):
                chunk = chunk_of(behind(k), half)

                @pl.when(needs(me, chunk))
                def _(k=k, half=half, chunk=chunk):
                    gather_copy(g, k, half, chunk).wait_recv()

        for half in range(2):
            bias = bias_a if half == 0 else bias_b
            size = bias.shape[0]
            count = size // half_rows
            window = pl.ds(0 if half == 0 else first_b, count)
            low, high = half * half_rows, (half + 1) * half_rows
            keys = kv[g, window, 0].reshape(size, HEAD_SIZE)
            values = kv[g, window, 1].reshape(size, HEAD_SIZE)
            queries = jnp.concatenate(stacked(q, g, half), axis=0)
            grads = jnp.concatenate(
                [(c.astype(f32) * live_rows[low:high, :]).astype(bf16)
                 for c in stacked(cot, g, half)],
                axis=0,
            )
            scores = matmul_nt(keys, queries) * score_scale + bias[...]
            peak = jnp.max(scores, axis=0, keepdims=True)
            mass = jnp.exp(scores - peak)
            total = jnp.sum(mass, axis=0, keepdims=True)
            weights = mass * (1.0 / total)
            rounded = weights.astype(bf16)
            out_t = matmul(jnp.transpose(values), rounded).astype(bf16).astype(f32)
            delta = jnp.sum(jnp.transpose(grads.astype(f32)) * out_t, axis=0, keepdims=True)
            out = jnp.transpose(out_t).astype(bf16)
            pushes = matmul_nt(values, grads)
            slopes = (weights * (pushes - delta) * score_scale).astype(bf16)
            rows_t = matmul(jnp.transpose(keys), slopes)
            grad_rows = jnp.transpose(rows_t)
            for j in range(heads):
                columns = pl.ds(j * HEAD_SIZE, HEAD_SIZE)
                wide = pl.ds(pl.multiple_of(g * width + j * HEAD_SIZE, HEAD_SIZE), HEAD_SIZE)
                att[low:high, wide] = out[j * half_rows:(j + 1) * half_rows, :]
                gq32[g, low:high, columns] = grad_rows[j * half_rows:(j + 1) * half_rows, :]
            key_part = matmul(slopes, queries).reshape(count, half_rows, HEAD_SIZE)
            value_part = matmul(rounded, grads).reshape(count, half_rows, HEAD_SIZE)
            if half == 0:
                rest = jnp.zeros((chunks - count, half_rows, HEAD_SIZE), f32)
                acc_k[0:count] = key_part
                acc_v[0:count] = value_part
                acc_k[count:] = rest
                acc_v[count:] = rest
            else:
                acc_k[window] += key_part
                acc_v[window] += value_part
        tx[g, :, 0] = acc_k[...].astype(bf16)
        tx[g, :, 1] = acc_v[...].astype(bf16)
        for k in far_first:
            for half in range(2):
                chunk = chunk_of(ahead(k), half)

                @pl.when(needs(me, chunk))
                def _(k=k, half=half, chunk=chunk):
                    scatter_copy(g, k, half, chunk).start()

        for stage in range(1, stages + 1):

            @pl.when(g == min(stage - 1, groups - 1))
            def _(stage=stage):
                live_stage(stage)

        return carry

    lax.fori_loop(0, groups, group_step, 0)

    count = jnp.sum(live2[stages].astype(f32), axis=1, keepdims=True)
    ratio = float(depth * n * rows) / count

    def scale_step(g, carry):
        wide = pl.ds(pl.multiple_of(g * width, width), width)
        gq[:, wide] = (gq32[g] * ratio).astype(bf16)
        return carry

    lax.fori_loop(0, groups, scale_step, 0)

    def reduce_step(g, carry):
        columns = pl.ds(pl.multiple_of(g * HEAD_SIZE, HEAD_SIZE), HEAD_SIZE)
        for half in range(2):
            mine = chunk_of(me, half)
            low, high = half * half_rows, (half + 1) * half_rows
            acc_k[0] = tx[g, mine, 0].astype(f32)
            acc_v[0] = tx[g, mine, 1].astype(f32)
            for k in range(1, n):

                @pl.when(needs(behind(k), mine))
                def _(k=k, half=half):
                    scatter_copy(g, k, half, mine).wait_recv()
                    acc_k[0] += rx[g, k, half, 0].astype(f32)
                    acc_v[0] += rx[g, k, half, 1].astype(f32)

            kg_ref[low:high, columns] = (acc_k[0] * ratio).astype(bf16)
            vg_ref[low:high, columns] = (acc_v[0] * ratio).astype(bf16)
        return carry

    lax.fori_loop(0, groups, reduce_step, 0)

    def drain(g, carry):
        for k in range(1, n):
            for half in range(2):
                mine, theirs = chunk_of(me, half), chunk_of(ahead(k), half)

                @pl.when(needs(ahead(k), mine))
                def _(k=k, half=half):
                    gather_copy(g, k, half, mine).wait_send()

                @pl.when(needs(me, theirs))
                def _(k=k, half=half):
                    scatter_copy(g, k, half, theirs).wait_send()

        return carry

    lax.fori_loop(0, groups, drain, 0)


def store_kernel(*refs):
    sources, targets, sem = refs[:4], refs[4:8], refs[8]
    copies = [
        pltpu.make_async_copy(source, target, sem.at[i])
        for i, (source, target) in enumerate(zip(sources, targets))
    ]
    for copy in copies:
        copy.start()
    for copy in copies:
        copy.wait()


def on_device(n, depth, queries, keys, values, cotangent, live, docs):
    rows, q_width = queries.shape[1:]
    kv_width = keys.shape[2]
    groups = kv_width // HEAD_SIZE
    width = q_width // groups
    heads = width // HEAD_SIZE
    half_rows = rows // 2
    chunks = 2 * n
    lanes = heads * half_rows
    anywhere = pl.BlockSpec(memory_space=pl.ANY)
    vmem = pl.BlockSpec(memory_space=pltpu.VMEM)
    dma = pltpu.SemaphoreType.DMA
    block = (2, half_rows, HEAD_SIZE)
    shapes = ((rows, q_width),) * 2 + ((rows, kv_width),) * 2
    stages = depth.bit_length() - 1
    if depth != 1 << stages:
        raise ValueError("dp size")
    results = pl.pallas_call(
        functools.partial(kernel, n, depth),
        out_shape=tuple(pltpu.VMEM(shape, bf16) for shape in shapes),
        in_specs=[anywhere] * 5 + [vmem],
        out_specs=(vmem,) * 4,
        scratch_shapes=[
            pltpu.VMEM((rows, q_width), bf16),
            pltpu.VMEM((rows, q_width), bf16),
            pltpu.VMEM((groups, chunks) + block, bf16),
            pltpu.VMEM((groups, chunks) + block, bf16),
            pltpu.VMEM((groups, n, 2) + block, bf16),
            pltpu.VMEM((groups, rows, width), f32),
            pltpu.VMEM((chunks, half_rows, HEAD_SIZE), f32),
            pltpu.VMEM((chunks, half_rows, HEAD_SIZE), f32),
            pltpu.VMEM((n * half_rows, lanes), f32),
            pltpu.VMEM(((n + 2) * half_rows, lanes), f32),
            pltpu.VMEM((n * rows, HEAD_SIZE), f32),
            pltpu.VMEM((rows, HEAD_SIZE), f32),
            pltpu.VMEM((n, 1, rows), jnp.int32),
            pltpu.VMEM((stages + 1, 1, rows), jnp.int32),
            pltpu.VMEM((max(stages, 1), 1, rows), jnp.int32),
            dma((3,)),
            dma((groups, 2, 2)),
            dma((groups, n, 2)),
            dma((groups, n, 2)),
            dma((groups, n, 2)),
            dma((groups, n, 2)),
            dma((n,)),
            dma((n,)),
            dma((max(stages, 1),)),
            dma((max(stages, 1),)),
        ],
        compiler_params=pltpu.CompilerParams(
            collective_id=0, has_side_effects=True, vmem_limit_bytes=60 * 1024 * 1024
        ),
    )(queries[0], keys[0], values[0], cotangent[0], live, docs)
    outputs = pl.pallas_call(
        store_kernel,
        out_shape=tuple(jax.ShapeDtypeStruct(shape, bf16) for shape in shapes),
        in_specs=[vmem] * 4,
        out_specs=(anywhere,) * 4,
        scratch_shapes=[dma((4,))],
        compiler_params=pltpu.CompilerParams(vmem_limit_bytes=16 * 1024 * 1024),
    )(*results)
    return tuple(output[None] for output in outputs)


def solution(mesh):
    wide = P("dp", "ctx", None)
    return jax.shard_map(
        functools.partial(on_device, mesh.shape["ctx"], mesh.shape["dp"]),
        mesh=mesh,
        in_specs=(wide, wide, wide, wide, P("dp", "ctx"), P("dp", None)),
        out_specs=(wide, wide, wide, wide),
        check_vma=False,
    )
```
